32 devices in a mesh: gx: 8 (over z, x), gy: 4 (over y, core).
Axes of the slice: x: 2, y: 2, z: 4, core: 2. Of those that a mesh axis runs over, the one named last changes fastest.
Arguments:
- velocity_x: float32 [1024, 4, 384], P('gx', 'gy'), may hold values from -6 to 6
- velocity_z: float32 [1024, 4, 384], P('gx', 'gy'), may hold values from -6 to 6
- stress_xx: float32 [1024, 4, 384], P('gx', 'gy'), may hold values from -6 to 6
- stress_zz: float32 [1024, 4, 384], P('gx', 'gy'), may hold values from -6 to 6
- stress_xz: float32 [1024, 4, 384], P('gx', 'gy'), may hold values from -6 to 6
- material: int32 [1024, 4, 384], P('gx', 'gy'), may hold values from 0 to 15, as said below
- land_mask: int32 [1024, 4], P('gx', 'gy'), may hold values 0 or 1
- density: float32 [16], replicated, may hold values from 1 to 3
- lame_lambda: float32 [16], replicated, may hold values from 0.5 to 4
- shear_modulus: float32 [16], replicated, may hold values from 0.3 to 2
- continuation_land: float32 [26, 27], replicated, may hold values from -1.25 to 1.25
- continuation_sea: float32 [26, 27], replicated, may hold values from -1.25 to 1.25
- continuation_bottom: float32 [26, 27], replicated, may hold values from -1.25 to 1.25
Outputs:
- next_velocity_x: float32 [1024, 4, 384], P('gx', 'gy')
- next_velocity_z: float32 [1024, 4, 384], P('gx', 'gy')
- next_stress_xx: float32 [1024, 4, 384], P('gx', 'gy')
- next_stress_zz: float32 [1024, 4, 384], P('gx', 'gy')
- next_stress_xz: float32 [1024, 4, 384], P('gx', 'gy')
The draws below stay inside these ranges and needn't reach their ends.
Inputs may be any that keep to these rules, and one draw needn't show every extreme that they name: `material`: in every vertical line the layer number never falls with depth, and it is 0 at depth index 0.
All inputs are finite; a program needn't handle non-finite values. No bound on the sum of `land_mask` on one device may be relied on, other than what follows from the above.
Results may differ from the reference program's by a relative error of at most 0.000073.
Values sent between devices are 32-bit elements; how exact they have to be, the bound alone decides.
No kernel may reach another device: no remote copies, remote signals or barrier semaphores. Data moves between devices by JAX's collectives and lax.ppermute only.
A program may use at most 64 MiB of HBM per device.

```python
import math
import jax
import jax.numpy as jnp
from jax import lax

NX = 1024
NZ = 384
LAYERS = 16
WINDOW = 27
CONT = 26
SECTIONS = 4


def draw_material(key, part):
    thickness = jax.random.randint(key, (LAYERS - 1, NX, SECTIONS), 1, 2 * NZ // LAYERS)
    levels = lax.broadcasted_iota(jnp.int32, (NX, SECTIONS, NZ), 2)
    interface = jnp.zeros((NX, SECTIONS), jnp.int32)
    strata = jnp.zeros((NX, SECTIONS, NZ), jnp.int32)
    for boundary_index in range(LAYERS - 1):
        interface = interface + thickness[boundary_index]
        strata = strata + (levels >= interface[:, :, None]).astype(jnp.int32)
    return strata


def plant(drawn, stream_key, smallest, largest):
    longest = drawn.shape.index(max(drawn.shape))
    spots = []
    for shift in (0, 1):
        where = [jax.random.randint(jax.random.fold_in(stream_key, axis), (), 0, length) for axis, length in enumerate(drawn.shape)]
        where[longest] = (where[longest] + shift) % drawn.shape[longest]
        spots.append(tuple(where))
    return drawn.at[spots[0]].set(smallest).at[spots[1]].set(largest)


def block_scale(key, extent, shards, smallest, top_value):
    factor_of, own = 1.0, jax.random.fold_in(key, 6)
    for dim, parts in shards:
        heights = jnp.exp(jax.random.uniform(jax.random.fold_in(own, dim), (parts,), jnp.float32, smallest / len(shards), top_value / len(shards)))
        factor_of = factor_of * jnp.repeat(heights, extent[dim] // parts).reshape([-1 if axis == dim else 1 for axis in range(len(extent))])
    return factor_of


def gaussian(own_key, dims, spread, most, cuts=(), held_as=jnp.bfloat16):
    entries = spread * jax.random.normal(own_key, dims, jnp.float32)
    if cuts:
        entries = entries * block_scale(own_key, dims, cuts, -0.22, 0.18)
    return jnp.clip(entries, -most, most).astype(held_as)


def setup_inputs(seed: int = 0) -> dict:
    key_list = jax.random.split(jax.random.key(seed), 14)
    velocity_x = gaussian(key_list[0], (NX, SECTIONS, NZ), 1.0, 6.0, ((0, 8), (1, 4)), jnp.float32)
    velocity_z = gaussian(key_list[1], (NX, SECTIONS, NZ), 1.0, 6.0, ((0, 8), (1, 4)), jnp.float32)
    stress_xx = gaussian(key_list[2], (NX, SECTIONS, NZ), 1.0, 6.0, ((0, 8), (1, 4)), jnp.float32)
    stress_zz = gaussian(key_list[3], (NX, SECTIONS, NZ), 1.0, 6.0, ((0, 8), (1, 4)), jnp.float32)
    stress_xz = gaussian(key_list[4], (NX, SECTIONS, NZ), 1.0, 6.0, ((0, 8), (1, 4)), jnp.float32)
    material = draw_material(jax.random.fold_in(key_list[13], 71), 0)
    land_mask = plant((jax.random.randint(key_list[6], (NX, SECTIONS), 0, 2) < 1).astype(jnp.int32), jax.random.fold_in(key_list[6], 1), 0, 1)
    density = jnp.clip(jnp.exp(jax.random.uniform(key_list[7], (LAYERS,), jnp.float32, math.log(1.0), math.log(3.0))), 1.0, 3.0)
    lame_lambda = jnp.clip(jnp.exp(jax.random.uniform(key_list[8], (LAYERS,), jnp.float32, math.log(0.5), math.log(4.0))), 0.5, 4.0)
    shear_modulus = jnp.clip(jnp.exp(jax.random.uniform(key_list[9], (LAYERS,), jnp.float32, math.log(0.3), math.log(2.0))), 0.3, 2.0)
    continuation_land = gaussian(key_list[10], (CONT, WINDOW), WINDOW ** -0.5, 1.25, (), jnp.float32)
    continuation_sea = gaussian(key_list[11], (CONT, WINDOW), WINDOW ** -0.5, 1.25, (), jnp.float32)
    continuation_bottom = gaussian(key_list[12], (CONT, WINDOW), WINDOW ** -0.5, 1.25, (), jnp.float32)
    return dict(velocity_x=velocity_x, velocity_z=velocity_z, stress_xx=stress_xx, stress_zz=stress_zz, stress_xz=stress_xz, material=material, land_mask=land_mask, density=density, lame_lambda=lame_lambda, shear_modulus=shear_modulus, continuation_land=continuation_land, continuation_sea=continuation_sea, continuation_bottom=continuation_bottom)


time_step = 0.2
highest = lax.Precision.HIGHEST


def spectral(length):
    indices = jnp.arange(length, dtype=jnp.int32)
    distance = jnp.mod(indices[:, None] - indices[None, :] + length // 2, length) - length // 2
    parity = 1.0 - 2.0 * jnp.mod(distance, 2).astype(jnp.float32)
    angles = jnp.pi * distance.astype(jnp.float32) / length
    tangent = jnp.where(distance == 0, 1.0, jnp.tan(angles))
    return jnp.where(distance == 0, 0.0, parity * (jnp.pi / length) / tangent)


def product(left, right):
    return jnp.dot(left, right, precision=highest, preferred_element_type=jnp.float32)


def reference(velocity_x, velocity_z, stress_xx, stress_zz, stress_xz, material, land_mask, density, lame_lambda, shear_modulus, continuation_land, continuation_sea, continuation_bottom):
    across_matrix = spectral(NX)
    depth_matrix = spectral(NZ + CONT)
    interior_t = depth_matrix[:NZ, :NZ].T
    boundary_t = depth_matrix[:NZ, NZ:].T
    land_rows = land_mask.reshape(-1, 1) > 0

    def lateral(quantity):
        return product(across_matrix, quantity.reshape(NX, -1)).reshape(quantity.shape)

    def vertical(quantity):
        lines = quantity.reshape(-1, NZ)
        upper = lines[:, :WINDOW]
        lower = lines[:, NZ - WINDOW:]
        extension = jnp.where(land_rows, product(upper, continuation_land.T), product(upper, continuation_sea.T)) + product(lower, continuation_bottom.T)
        return (product(lines, interior_t) + product(extension, boundary_t)).reshape(quantity.shape)

    buoyancy = 1.0 / density[material]
    lame_first = lame_lambda[material]
    shear_coef = shear_modulus[material]
    next_velocity_x = velocity_x + time_step * buoyancy * (lateral(stress_xx) + vertical(stress_xz))
    next_velocity_z = velocity_z + time_step * buoyancy * (lateral(stress_xz) + vertical(stress_zz))
    lateral_vx = lateral(next_velocity_x)
    lateral_vz = lateral(next_velocity_z)
    depth_vx = vertical(next_velocity_x)
    depth_vz = vertical(next_velocity_z)
    normal_coef = lame_first + 2.0 * shear_coef
    next_stress_xx = stress_xx + time_step * (normal_coef * lateral_vx + lame_first * depth_vz)
    next_stress_zz = stress_zz + time_step * (lame_first * lateral_vx + normal_coef * depth_vz)
    next_stress_xz = stress_xz + time_step * shear_coef * (depth_vx + lateral_vz)
    surface = lax.broadcasted_iota(jnp.int32, (1, 1, NZ), 2) == 0
    next_stress_zz = jnp.where(surface & (land_mask[:, :, None] > 0), 0.0, next_stress_zz)
    next_stress_xz = jnp.where(surface, 0.0, next_stress_xz)
    return next_velocity_x, next_velocity_z, next_stress_xx, next_stress_zz, next_stress_xz
```

```python
import functools

import jax
import jax.numpy as jnp
import numpy as np
from jax import lax
from jax.experimental import pallas as pl
from jax.experimental.pallas import tpu as pltpu
from jax.sharding import PartitionSpec as P

time_step = 0.2
LANES = 128
VMEM = pl.BlockSpec(memory_space=pltpu.VMEM)
SMEM = pl.BlockSpec(memory_space=pltpu.SMEM)


def circulant_row(length):
    m = np.arange(length)
    m = np.where(m < length - length // 2, m, m - length)
    angle = np.pi * m / length
    tangent = np.where(m == 0, 1.0, np.tan(angle))
    return np.where(m == 0, 0.0, (1.0 - 2.0 * (m % 2)) * (np.pi / length) / tangent)


def halves(matrix):
    matrix = matrix.astype(np.float32)
    high = matrix.astype(jnp.bfloat16)
    low = (matrix - high.astype(np.float32)).astype(jnp.bfloat16)
    return jnp.asarray(np.stack([high, low]))


def lateral_constants(length):
    c = circulant_row(length)

    def block(first, second, sign, scale):
        n = len(first)
        d = np.arange(n)[None, :] - np.arange(n)[:, None]
        value = first + sign * second
        entry = value[d % n]
        return scale * (entry if sign > 0 else np.where(d < 0, -entry, entry))

    h = length // 2
    skew_half = block(c[:h], c[h:], -1, 0.5)
    u = c[:h] + c[h:]
    q = h // 2
    return (
        halves(block(u[:q], u[q:], 1, 0.25)),
        halves(block(u[:q], u[q:], -1, 0.25)),
        halves(skew_half),
    )


def depth_constants(depth, extra):
    c = circulant_row(depth + extra)
    j, k = np.arange(depth), np.arange(depth + extra)
    matrix = c[(j[:, None] - k[None, :]) % (depth + extra)]
    pad = -(-extra // 32) * 32
    boundary = np.zeros((pad, depth))
    boundary[:extra] = matrix[:, depth:].T
    return halves(matrix[:, :depth].T), halves(boundary)


def split(x):
    high = x.astype(jnp.bfloat16)
    return high, (x - high.astype(jnp.float32)).astype(jnp.bfloat16)


def times(x, right):
    high, low = split(x)

    def mm(a, b):
        return jnp.dot(a, b, preferred_element_type=jnp.float32)

    return mm(high, right[0]) + (mm(low, right[0]) + mm(high, right[1]))


def times_t(x, left):
    high, low = split(x)
    left_high, left_low = split(left)

    def mm(a, b):
        return lax.dot_general(a, b, (((1,), (1,)), ((), ())), preferred_element_type=jnp.float32)

    return mm(high, left_high) + (mm(low, left_high) + mm(high, left_low))


def fold(x):
    h = x.shape[1] // 2
    return x[:, :h] + x[:, h:], x[:, :h] - x[:, h:]


def unfold(a, b):
    return jnp.concatenate([a + b, a - b], axis=1)


def lateral(x, even_ref, odd_ref, skew_ref):
    u, w = fold(x)
    uu, uw = fold(u)
    return unfold(unfold(times(uu, even_ref), times(uw, odd_ref)), times(w, skew_ref))


def lines_of(ref, lines):
    chunks = ref.shape[0] // lines
    return [ref[pl.ds(c, lines, stride=chunks), :] for c in range(chunks)]


def put_lines(ref, chunks):
    for c, value in enumerate(chunks):
        ref[pl.ds(c, value.shape[0], stride=len(chunks)), :] = value


def turned(chunks):
    return jnp.concatenate([v.T for v in chunks], axis=0)


def send_rows(ref, first, field):
    w = field.shape[0] // ref.shape[0]
    for d in range(ref.shape[0]):
        ref[d, first : first + w, :] = field[d * w : (d + 1) * w]


def look_up(material, table_ref):
    value = jnp.full(material.shape, table_ref[0], jnp.float32)
    for layer in range(1, table_ref.shape[0]):
        value = jnp.where(material >= layer, table_ref[layer], value)
    return value


def depth_pair(first, second, land, gram_ref, inner_ref, outer_ref):
    lines = first[0].shape[0]
    both = jnp.concatenate(
        [jnp.concatenate(first, axis=1), jnp.concatenate(second, axis=1)], axis=0
    )
    pad = outer_ref.shape[1]
    top = times_t(both[:, :LANES], gram_ref[: 2 * pad])
    bottom = times_t(both[:, both.shape[1] - LANES :], gram_ref[2 * pad :])
    picked = jnp.concatenate([land, land], axis=0)[:, :pad]
    extension = jnp.where(picked, top[:, :pad], top[:, pad:]) + bottom
    out = times(both, inner_ref) + times(extension, outer_ref)

    def chunked(x):
        return [x[:, c * LANES : (c + 1) * LANES] for c in range(len(first))]

    return chunked(out[:lines]), chunked(out[lines:])


def land_of(land_ref):
    lines = land_ref.shape[1]
    return jnp.broadcast_to(land_ref[...], (LANES, lines)).T > 0


def send_kernel(xx_ref, xz_ref, out_ref):
    lines = out_ref.shape[2]
    w = out_ref.shape[1] // 2
    send_rows(out_ref, 0, turned(lines_of(xx_ref, lines)))
    send_rows(out_ref, w, turned(lines_of(xz_ref, lines)))


def middle_kernel(
    step_ref, xz_ref, zz_ref, vx_ref, vz_ref, material_ref, land_ref, gram_ref, inner_ref, outer_ref, out_ref
):
    lines = land_ref.shape[1]
    groups = out_ref.shape[0]
    layers = step_ref.shape[0]
    material = lines_of(material_ref, lines)
    depth_xz, depth_zz = depth_pair(
        lines_of(xz_ref, lines), lines_of(zz_ref, lines), land_of(land_ref), gram_ref, inner_ref, outer_ref
    )
    step = [look_up(m, step_ref) for m in material]
    w = material_ref.shape[0] * LANES // lines // groups
    for first, v_ref, d in ((0, vx_ref, depth_xz), (w, vz_ref, depth_zz)):
        mixed = [v + s * x for v, s, x in zip(lines_of(v_ref, lines), step, d)]
        send_rows(out_ref, first, turned(mixed))
    down = turned(material)
    counts = [
        jnp.sum((down < layer).astype(jnp.float32), axis=0, keepdims=True) for layer in range(1, layers)
    ]
    rows = out_ref.shape[1] - 2 * w
    counts = jnp.concatenate(counts + [counts[-1]] * (rows - layers + 1), axis=0)
    for d in range(groups):
        out_ref[d, 2 * w :, :] = counts


def lateral_kernel(in_ref, even_ref, odd_ref, skew_ref, out_ref):
    x = jnp.concatenate([in_ref[q] for q in range(in_ref.shape[0])], axis=1)
    y = lateral(x, even_ref, odd_ref, skew_ref)
    n = in_ref.shape[2]
    for q in range(out_ref.shape[0]):
        out_ref[q] = y[:, q * n : (q + 1) * n]


def velocity_kernel(place_ref, step_ref, lateral_ref, mixed_ref, out_ref):
    groups, rows, n = lateral_ref.shape
    w = rows // 2
    depth = (lax.broadcasted_iota(jnp.int32, (w, n), 0) + place_ref[0] * w).astype(jnp.float32)
    for q in range(groups):
        step = jnp.full((w, n), step_ref[0], jnp.float32)
        for layer in range(1, step_ref.shape[0]):
            interface = mixed_ref[q, rows + layer - 1 : rows + layer, :]
            step = jnp.where(depth >= interface, step_ref[layer], step)
        for first in (0, w):
            out_ref[q, first : first + w, :] = (
                mixed_ref[q, first : first + w, :] + step * lateral_ref[q, first : first + w, :]
            )


def gather_rows(ref, first, w):
    field = jnp.concatenate([ref[d, first : first + w, :] for d in range(ref.shape[0])], axis=0)
    return [field[c * LANES : (c + 1) * LANES].T for c in range(field.shape[0] // LANES)]


def depth_kernel(
    v_ref, land_ref, gram_ref, inner_ref, outer_ref, vx_ref, vz_ref, dx_ref, dz_ref
):
    w = v_ref.shape[1] // 2
    vx, vz = gather_rows(v_ref, 0, w), gather_rows(v_ref, w, w)
    put_lines(vx_ref, vx)
    put_lines(vz_ref, vz)
    dx, dz = depth_pair(vx, vz, land_of(land_ref), gram_ref, inner_ref, outer_ref)
    put_lines(dx_ref, dx)
    put_lines(dz_ref, dz)


def stress_kernel(
    lame_ref, shear_ref, in_ref, dx_ref, dz_ref, material_ref, land_ref, xx_ref, zz_ref, xz_ref,
    new_xx_ref, new_zz_ref, new_xz_ref,
):
    lines = land_ref.shape[1]
    w = in_ref.shape[1] // 2
    lateral_x, lateral_z = gather_rows(in_ref, 0, w), gather_rows(in_ref, w, w)
    land = land_of(land_ref)
    chunks = len(lateral_x)
    results = ([], [], [])
    dx, dz = lines_of(dx_ref, lines), lines_of(dz_ref, lines)
    xx, zz, xz = lines_of(xx_ref, lines), lines_of(zz_ref, lines), lines_of(xz_ref, lines)
    material = lines_of(material_ref, lines)
    for c in range(chunks):
        lame = look_up(material[c], lame_ref)
        shear = look_up(material[c], shear_ref)
        normal = lame + 2.0 * shear
        new_xx = xx[c] + time_step * (normal * lateral_x[c] + lame * dz[c])
        new_zz = zz[c] + time_step * (lame * lateral_x[c] + normal * dz[c])
        new_xz = xz[c] + time_step * shear * (dx[c] + lateral_z[c])
        if c == 0:
            surface = lax.broadcasted_iota(jnp.int32, new_zz.shape, 1) == 0
            new_zz = jnp.where(surface & land, 0.0, new_zz)
            new_xz = jnp.where(surface, 0.0, new_xz)
        for kept, value in zip(results, (new_xx, new_zz, new_xz)):
            kept.append(value)
    for ref, value in zip((new_xx_ref, new_zz_ref, new_xz_ref), results):
        put_lines(ref, value)


def call(kernel, outs, specs, args, flops, name):
    moved = sum(a.size * a.dtype.itemsize for a in (*args, *outs))
    single = len(outs) == 1
    return pl.pallas_call(
        kernel,
        out_shape=outs[0] if single else tuple(outs),
        in_specs=list(specs),
        out_specs=VMEM if single else (VMEM,) * len(outs),
        cost_estimate=pl.CostEstimate(flops=flops, bytes_accessed=moved, transcendentals=0),
        compiler_params=pltpu.CompilerParams(vmem_limit_bytes=40 << 20),
        name=name,
    )(*args)


def exchange(x):
    return lax.all_to_all(x, "gx", split_axis=0, concat_axis=0, tiled=True)


def body(
    groups,
    velocity_x,
    velocity_z,
    stress_xx,
    stress_zz,
    stress_xz,
    material,
    land_mask,
    density,
    lame_lambda,
    shear_modulus,
    continuation_land,
    continuation_sea,
    continuation_bottom,
):
    lines, _, depth = velocity_x.shape
    width = lines * groups
    extra, window = continuation_land.shape
    layers = density.shape[0]
    w = depth // groups
    f32 = jnp.float32

    def shape(*dims):
        return jax.ShapeDtypeStruct(dims, f32)

    def flat(x):
        return x.reshape(lines * depth // LANES, LANES)

    vx, vz, xx, zz, xz, material = map(
        flat, (velocity_x, velocity_z, stress_xx, stress_zz, stress_xz, material)
    )
    land = land_mask.reshape(1, lines)
    inner, outer = depth_constants(depth, extra)
    fold_matrices = lateral_constants(width)
    pad = outer.shape[1]

    def padded(g, start):
        return jnp.pad(g, ((0, pad - extra), (start, LANES - window - start)))

    gram = jnp.concatenate(
        [padded(continuation_land, 0), padded(continuation_sea, 0), padded(continuation_bottom, LANES - window)],
        axis=0,
    )
    step = time_step * (1.0 / density)
    place = lax.axis_index("gx").astype(jnp.int32).reshape(1)
    rows = -(-(layers - 1) // 8) * 8
    depth_flops = 2 * 2 * lines * depth * depth * 3
    lateral_flops = 2 * 2 * w * width * width

    packed = call(
        send_kernel, [shape(groups, 2 * w, lines)], [VMEM] * 2, (xx, xz), 1 << 20, "send"
    )
    arrived = exchange(packed)
    mixed = call(
        middle_kernel,
        [shape(groups, 2 * w + rows, lines)],
        [SMEM] + [VMEM] * 9,
        (step, xz, zz, vx, vz, material, land, gram, inner, outer),
        depth_flops,
        "middle",
    )
    mixed = exchange(mixed)
    slopes = call(
        lateral_kernel,
        [shape(groups, 2 * w, lines)],
        [VMEM] * 4,
        (arrived, *fold_matrices),
        lateral_flops,
        "lateral_stress",
    )
    moving = call(
        velocity_kernel,
        [shape(groups, 2 * w, lines)],
        [SMEM, SMEM, VMEM, VMEM],
        (place, step, slopes, mixed),
        1 << 20,
        "velocity",
    )
    settled = exchange(moving)
    slopes = call(
        lateral_kernel,
        [shape(groups, 2 * w, lines)],
        [VMEM] * 4,
        (moving, *fold_matrices),
        lateral_flops,
        "lateral_velocity",
    )
    slopes = exchange(slopes)
    like = jax.ShapeDtypeStruct(vx.shape, f32)
    next_vx, next_vz, depth_vx, depth_vz = call(
        depth_kernel,
        [like] * 4,
        [VMEM] * 5,
        (settled, land, gram, inner, outer),
        depth_flops,
        "depth",
    )
    next_xx, next_zz, next_xz = call(
        stress_kernel,
        [like] * 3,
        [SMEM, SMEM] + [VMEM] * 8,
        (lame_lambda, shear_modulus, slopes, depth_vx, depth_vz, material, land, xx, zz, xz),
        1 << 20,
        "stress",
    )
    return tuple(
        x.reshape(velocity_x.shape) for x in (next_vx, next_vz, next_xx, next_zz, next_xz)
    )


def solution(mesh):
    field = P("gx", "gy", None)
    return jax.shard_map(
        functools.partial(body, mesh.shape["gx"]),
        mesh=mesh,
        in_specs=(field,) * 6 + (P("gx", "gy"),) + (P(),) * 6,
        out_specs=(field,) * 5,
        check_vma=False,
    )
```

```python
import functools

import jax
import jax.numpy as jnp
import numpy as np
from jax import lax
from jax.experimental import pallas as pl
from jax.experimental.pallas import tpu as pltpu
from jax.sharding import PartitionSpec as P


time_step = 0.2
LANES = 128
VMEM = pl.BlockSpec(memory_space=pltpu.VMEM)
SMEM = pl.BlockSpec(memory_space=pltpu.SMEM)
HBM = pl.BlockSpec(memory_space=pltpu.HBM)


def circulant_row(length):
    m = np.arange(length)
    m = np.where(m < length - length // 2, m, m - length)
    angle = np.pi * m / length
    tangent = np.where(m == 0, 1.0, np.tan(angle))
    return np.where(m == 0, 0.0, (1.0 - 2.0 * (m % 2)) * (np.pi / length) / tangent)


def halves(matrix):
    matrix = matrix.astype(np.float32)
    high = matrix.astype(jnp.bfloat16)
    low = (matrix - high.astype(np.float32)).astype(jnp.bfloat16)
    return jnp.asarray(np.stack([high, low]))


def lateral_constants(length):
    c = circulant_row(length)

    def block(first, second, sign, scale):
        n = len(first)
        d = np.arange(n)[None, :] - np.arange(n)[:, None]
        value = first + sign * second
        entry = value[d % n]
        return scale * (entry if sign > 0 else np.where(d < 0, -entry, entry))

    h = length // 2
    skew_half = block(c[:h], c[h:], -1, 0.5)
    u = c[:h] + c[h:]
    q = h // 2
    return (
        halves(block(u[:q], u[q:], 1, 0.25)),
        halves(block(u[:q], u[q:], -1, 0.25)),
        halves(skew_half),
    )


def depth_constants(depth, extra):
    c = circulant_row(depth + extra)
    j, k = np.arange(depth), np.arange(depth + extra)
    matrix = c[(j[:, None] - k[None, :]) % (depth + extra)]
    pad = -(-extra // 32) * 32
    boundary = np.zeros((pad, depth))
    boundary[:extra] = matrix[:, depth:].T
    return halves(matrix[:, :depth].T), halves(boundary)


def split(x):
    high = x.astype(jnp.bfloat16)
    return high, (x - high.astype(jnp.float32)).astype(jnp.bfloat16)


def times(x, right):
    high, low = split(x)

    def mm(a, b):
        return jnp.dot(a, b, preferred_element_type=jnp.float32)

    return mm(high, right[0]) + (mm(low, right[0]) + mm(high, right[1]))


def times_t(x, left):
    high, low = split(x)
    left_high, left_low = split(left)

    def mm(a, b):
        return lax.dot_general(a, b, (((1,), (1,)), ((), ())), preferred_element_type=jnp.float32)

    return mm(high, left_high) + (mm(low, left_high) + mm(high, left_low))


def fold(x):
    h = x.shape[1] // 2
    return x[:, :h] + x[:, h:], x[:, :h] - x[:, h:]


def unfold(a, b):
    return jnp.concatenate([a + b, a - b], axis=1)


def lateral(x, even_ref, odd_ref, skew_ref):
    u, w = fold(x)
    uu, uw = fold(u)
    return unfold(unfold(times(uu, even_ref), times(uw, odd_ref)), times(w, skew_ref))


def lines_of(ref, lines):
    chunks = ref.shape[0] // lines
    return [ref[pl.ds(c, lines, stride=chunks), :] for c in range(chunks)]


def put_lines(ref, chunks):
    for c, value in enumerate(chunks):
        ref[pl.ds(c, value.shape[0], stride=len(chunks)), :] = value


def turned(chunks):
    return jnp.concatenate([v.T for v in chunks], axis=0)


def send_rows(ref, first, field):
    w = field.shape[0] // ref.shape[0]
    for d in range(ref.shape[0]):
        ref[d, first : first + w, :] = field[d * w : (d + 1) * w]


def look_up(material, table_ref):
    value = jnp.full(material.shape, table_ref[0], jnp.float32)
    for layer in range(1, table_ref.shape[0]):
        value = jnp.where(material >= layer, table_ref[layer], value)
    return value


def depth_pair(first, second, land, gram, inner_ref, outer_ref):
    lines = first[0].shape[0]
    both = jnp.concatenate(
        [jnp.concatenate(first, axis=1), jnp.concatenate(second, axis=1)], axis=0
    )
    pad = outer_ref.shape[1]
    top = times_t(both[:, :LANES], gram[: 2 * pad])
    bottom = times_t(both[:, both.shape[1] - LANES :], gram[2 * pad :])
    picked = jnp.concatenate([land, land], axis=0)[:, :pad]
    extension = jnp.where(picked, top[:, :pad], top[:, pad:]) + bottom
    out = times(both, inner_ref) + times(extension, outer_ref)

    def chunked(x):
        return [x[:, c * LANES : (c + 1) * LANES] for c in range(len(first))]

    return chunked(out[:lines]), chunked(out[lines:])


def gram_of(top_land_ref, top_sea_ref, bottom_ref, pad):
    def padded(ref, start):
        extra, window = ref.shape
        return jnp.pad(ref[...], ((0, pad - extra), (start, LANES - window - start)))

    return jnp.concatenate(
        [padded(top_land_ref, 0), padded(top_sea_ref, 0), padded(bottom_ref, LANES - bottom_ref.shape[1])], axis=0
    )


def land_of(land_ref):
    lines = land_ref.shape[1]
    return jnp.broadcast_to(land_ref[...], (LANES, lines)).T > 0


def first_kernel(
    place_ref, xz_hbm, zz_hbm, inner_hbm, xx_hbm, material_hbm, vx_hbm, vz_hbm, land_hbm, top_land_hbm, top_sea_hbm,
    bottom_hbm, outer_hbm, density_hbm, *rest,
):
    (*out_refs, fields, material_ref, inner_ref, land_ref, top_land_ref, top_sea_ref, bottom_ref, outer_ref,
     density_ref, packed, sems) = rest
    groups = len(out_refs)
    lines = land_ref.shape[1]
    layers = density_ref.shape[0]
    moves = (
        (xz_hbm, fields.at[0]),
        (zz_hbm, fields.at[1]),
        (xx_hbm, fields.at[2]),
        (vx_hbm, fields.at[3]),
        (vz_hbm, fields.at[4]),
        (material_hbm, material_ref),
        (inner_hbm, inner_ref),
        (land_hbm, land_ref),
        (top_land_hbm, top_land_ref),
        (top_sea_hbm, top_sea_ref),
        (bottom_hbm, bottom_ref),
        (outer_hbm, outer_ref),
        (density_hbm, density_ref),
    )
    copies = [pltpu.make_async_copy(a, b, sems.at[i]) for i, (a, b) in enumerate(moves)]
    for i in (7, 8, 9, 10, 11, 12, 0, 1, 6, 2, 5, 3, 4):
        copies[i].start()
    for i in range(7, 13):
        copies[i].wait()
    gram = gram_of(top_land_ref, top_sea_ref, bottom_ref, outer_ref.shape[1])
    land = land_of(land_ref)
    w = fields.shape[1] * LANES // lines // groups
    copies[6].wait()
    copies[0].wait()
    copies[1].wait()
    xz = lines_of(fields.at[0], lines)
    depth_xz, depth_zz = depth_pair(
        xz, lines_of(fields.at[1], lines), land, gram, inner_ref, outer_ref
    )
    send_rows(packed, w, turned(xz))
    copies[2].wait()
    send_rows(packed, 0, turned(lines_of(fields.at[2], lines)))
    copies[5].wait()
    material = lines_of(material_ref, lines)
    down = turned(material)
    counts = [
        jnp.sum((down < layer).astype(jnp.float32), axis=0, keepdims=True) for layer in range(1, layers)
    ]
    rows = packed.shape[1] - 4 * w
    counts = jnp.concatenate(counts + [counts[-1]] * (rows - layers + 1), axis=0)
    for d in range(groups):
        packed[d, 4 * w :, :] = counts
    step = [time_step * (1.0 / look_up(m, density_ref)) for m in material]
    copies[3].wait()
    copies[4].wait()
    for first, i, d in ((2 * w, 3, depth_xz), (3 * w, 4, depth_zz)):
        mixed = [v + s * x for v, s, x in zip(lines_of(fields.at[i], lines), step, d)]
        send_rows(packed, first, turned(mixed))
    scatter_blocks(place_ref, packed, out_refs)


def scatter_blocks(place_ref, packed, out_refs):
    for s, ref in enumerate(out_refs):
        ref[...] = packed[place_ref[0] ^ s]


def collect_blocks(place_ref, in_refs, packed):
    for s, ref in enumerate(in_refs):
        packed[place_ref[0] ^ s] = ref[...]


def pencil_kernel(groups, place_ref, step_ref, even_ref, odd_ref, skew_ref, *rest):
    in_refs, out_refs, (arrived, leaving) = rest[:groups], rest[groups : 2 * groups], rest[2 * groups :]
    n = in_refs[0].shape[1]
    w = leaving.shape[1] // 4
    collect_blocks(place_ref, in_refs, arrived)
    x = jnp.concatenate([arrived[q, : 2 * w] for q in range(groups)], axis=1)
    slopes = lateral(x, even_ref, odd_ref, skew_ref)
    depth = (lax.broadcasted_iota(jnp.int32, (w, n), 0) + place_ref[0] * w).astype(jnp.float32)
    moving = []
    for q in range(groups):
        step = jnp.full((w, n), step_ref[0], jnp.float32)
        for layer in range(1, step_ref.shape[0]):
            interface = arrived[q, 4 * w + layer - 1 : 4 * w + layer, :]
            step = jnp.where(depth >= interface, step_ref[layer], step)
        step = jnp.concatenate([step, step], axis=0)
        new = arrived[q, 2 * w : 4 * w] + step * slopes[:, q * n : (q + 1) * n]
        leaving[q, : 2 * w] = new
        moving.append(new)
    slopes = lateral(jnp.concatenate(moving, axis=1), even_ref, odd_ref, skew_ref)
    for q in range(groups):
        leaving[q, 2 * w :] = slopes[:, q * n : (q + 1) * n]
    scatter_blocks(place_ref, leaving, out_refs)


def gather_rows(ref, first, w):
    field = jnp.concatenate([ref[d, first : first + w, :] for d in range(ref.shape[0])], axis=0)
    return [field[c * LANES : (c + 1) * LANES].T for c in range(field.shape[0] // LANES)]


def last_kernel(
    groups, place_ref, lame_ref, shear_ref, xx_ref, zz_ref, xz_ref, material_ref, land_ref,
    top_land_ref, top_sea_ref, bottom_ref, inner_ref, outer_ref, *rest,
):
    in_refs, (new_vx, new_vz, new_xx_ref, new_zz_ref, new_xz_ref, settled) = rest[:groups], rest[groups:]
    lines = land_ref.shape[1]
    w = settled.shape[1] // 4
    collect_blocks(place_ref, in_refs, settled)
    land = land_of(land_ref)
    gram = gram_of(top_land_ref, top_sea_ref, bottom_ref, outer_ref.shape[1])
    vx, vz, lateral_x, lateral_z = (gather_rows(settled, i * w, w) for i in range(4))
    put_lines(new_vx, vx)
    put_lines(new_vz, vz)
    dx, dz = depth_pair(vx, vz, land, gram, inner_ref, outer_ref)
    results = ([], [], [])
    xx, zz, xz = lines_of(xx_ref, lines), lines_of(zz_ref, lines), lines_of(xz_ref, lines)
    material = lines_of(material_ref, lines)
    for c in range(len(vx)):
        lame = look_up(material[c], lame_ref)
        shear = look_up(material[c], shear_ref)
        normal = lame + 2.0 * shear
        new_xx = xx[c] + time_step * (normal * lateral_x[c] + lame * dz[c])
        new_zz = zz[c] + time_step * (lame * lateral_x[c] + normal * dz[c])
        new_xz = xz[c] + time_step * shear * (dx[c] + lateral_z[c])
        if c == 0:
            surface = lax.broadcasted_iota(jnp.int32, new_zz.shape, 1) == 0
            new_zz = jnp.where(surface & land, 0.0, new_zz)
            new_xz = jnp.where(surface, 0.0, new_xz)
        for kept, value in zip(results, (new_xx, new_zz, new_xz)):
            kept.append(value)
    for ref, value in zip((new_xx_ref, new_zz_ref, new_xz_ref), results):
        put_lines(ref, value)


def call(kernel, outs, specs, args, flops, scratch=(), on_chip=True):
    moved = sum(a.size * a.dtype.itemsize for a in (*args, *outs))
    return pl.pallas_call(
        kernel,
        out_shape=tuple(pltpu.VMEM(o.shape, o.dtype) if on_chip else o for o in outs),
        in_specs=list(specs),
        out_specs=(VMEM,) * len(outs),
        scratch_shapes=list(scratch),
        cost_estimate=pl.CostEstimate(flops=flops, bytes_accessed=moved, transcendentals=0),
        compiler_params=pltpu.CompilerParams(vmem_limit_bytes=40 << 20),
    )(*args)


def hop_order(groups):
    return list(range(groups // 2, groups)) + list(range(groups // 2 - 1, 0, -1))


def exchange(blocks):
    groups = len(blocks)
    order = hop_order(groups)
    moved = {}
    for s in order:
        moved[s] = lax.ppermute(blocks[s], "gx", [(i, i ^ s) for i in range(groups)])
    return [blocks[0]] + [moved[s] for s in range(1, groups)]


def body(
    groups,
    velocity_x,
    velocity_z,
    stress_xx,
    stress_zz,
    stress_xz,
    material,
    land_mask,
    density,
    lame_lambda,
    shear_modulus,
    continuation_land,
    continuation_sea,
    continuation_bottom,
):
    lines, _, depth = velocity_x.shape
    width = lines * groups
    extra = continuation_land.shape[0]
    layers = density.shape[0]
    w = depth // groups
    f32 = jnp.float32

    def shape(*dims):
        return jax.ShapeDtypeStruct(dims, f32)

    def kept(x):
        return pltpu.with_memory_space_constraint(x, pltpu.HBM)

    def flat(x):
        return x.reshape(lines * depth // LANES, LANES)

    vx, vz, xx, zz, xz, material = map(
        flat, (velocity_x, velocity_z, stress_xx, stress_zz, stress_xz, material)
    )
    land = land_mask.reshape(1, lines)
    inner, outer = depth_constants(depth, extra)
    fold_matrices = lateral_constants(width)
    grams = (continuation_land, continuation_sea, continuation_bottom)
    step = time_step * (1.0 / density)
    place = lax.axis_index("gx").astype(jnp.int32).reshape(1)
    rows = -(-(layers - 1) // 8) * 8
    depth_flops = 2 * 2 * lines * depth * depth * 3
    lateral_flops = 2 * 2 * w * width * width
    stored = vx.shape

    leaving = call(
        first_kernel,
        [shape(4 * w + rows, lines)] * groups,
        [SMEM] + [HBM] * 13,
        (place, *map(kept, (xz, zz, inner, xx, material, vx, vz, land, *grams, outer, density))),
        depth_flops,
        [
            pltpu.VMEM((5, *stored), f32),
            pltpu.VMEM(stored, jnp.int32),
            pltpu.VMEM(inner.shape, inner.dtype),
            pltpu.VMEM(land.shape, jnp.int32),
            *(pltpu.VMEM(g.shape, f32) for g in grams),
            pltpu.VMEM(outer.shape, outer.dtype),
            pltpu.SMEM(density.shape, f32),
            pltpu.VMEM((groups, 4 * w + rows, lines), f32),
            pltpu.SemaphoreType.DMA((13,)),
        ],
    )
    arrived = exchange(leaving)
    leaving = call(
        functools.partial(pencil_kernel, groups),
        [shape(4 * w, lines)] * groups,
        [SMEM] * 2 + [VMEM] * (3 + groups),
        (place, step, *fold_matrices, *arrived),
        2 * lateral_flops,
        [
            pltpu.VMEM((groups, 4 * w + rows, lines), f32),
            pltpu.VMEM((groups, 4 * w, lines), f32),
        ],
    )
    arrived = exchange(leaving)
    results = call(
        functools.partial(last_kernel, groups),
        [shape(*stored)] * 5,
        [SMEM] * 3 + [VMEM] * (10 + groups),
        (place, lame_lambda, shear_modulus, xx, zz, xz, material, land, *grams, inner, outer, *arrived),
        depth_flops,
        [pltpu.VMEM((groups, 4 * w, lines), f32)],
        False,
    )
    return tuple(x.reshape(velocity_x.shape) for x in results)


def solution(mesh):
    field = P("gx", "gy", None)
    groups = mesh.shape["gx"]
    return jax.shard_map(
        functools.partial(body, groups),
        mesh=mesh,
        in_specs=(field,) * 6 + (P("gx", "gy"),) + (P(),) * 6,
        out_specs=(field,) * 5,
        check_vma=False,
    )
```

```python
import functools

import jax
import jax.numpy as jnp
import numpy as np
from jax import lax
from jax.experimental import pallas as pl
from jax.experimental.pallas import tpu as pltpu
from jax.sharding import PartitionSpec as P


time_step = 0.2
LANES = 128
VMEM = pl.BlockSpec(memory_space=pltpu.VMEM)
SMEM = pl.BlockSpec(memory_space=pltpu.SMEM)
HBM = pl.BlockSpec(memory_space=pltpu.HBM)


def circulant_row(length):
    m = np.arange(length)
    m = np.where(m < length - length // 2, m, m - length)
    angle = np.pi * m / length
    tangent = np.where(m == 0, 1.0, np.tan(angle))
    return np.where(m == 0, 0.0, (1.0 - 2.0 * (m % 2)) * (np.pi / length) / tangent)


def halves(matrix):
    matrix = matrix.astype(np.float32)
    high = matrix.astype(jnp.bfloat16)
    low = (matrix - high.astype(np.float32)).astype(jnp.bfloat16)
    return jnp.asarray(np.stack([high, low]))


def lateral_constants(length):
    c = circulant_row(length)

    def block(first, second, sign, scale):
        n = len(first)
        d = np.arange(n)[None, :] - np.arange(n)[:, None]
        value = first + sign * second
        entry = value[d % n]
        return scale * (entry if sign > 0 else np.where(d < 0, -entry, entry))

    h = length // 2
    skew_half = block(c[:h], c[h:], -1, 0.5)
    u = c[:h] + c[h:]
    q = h // 2
    return (
        halves(block(u[:q], u[q:], 1, 0.25)),
        halves(block(u[:q], u[q:], -1, 0.25)),
        halves(skew_half),
    )


def depth_constants(depth, extra):
    c = circulant_row(depth + extra)
    j, k = np.arange(depth), np.arange(depth + extra)
    matrix = c[(j[:, None] - k[None, :]) % (depth + extra)]
    pad = -(-extra // 32) * 32
    boundary = np.zeros((pad, depth))
    boundary[:extra] = matrix[:, depth:].T
    return halves(matrix[:, :depth].T), halves(boundary)


def split(x):
    high = x.astype(jnp.bfloat16)
    return high, (x - high.astype(jnp.float32)).astype(jnp.bfloat16)


def times(x, right):
    high, low = split(x)

    def mm(a, b):
        return jnp.dot(a, b, preferred_element_type=jnp.float32)

    return mm(high, right[0]) + (mm(low, right[0]) + mm(high, right[1]))


def times_t(x, left):
    high, low = split(x)
    left_high, left_low = split(left)

    def mm(a, b):
        return lax.dot_general(a, b, (((1,), (1,)), ((), ())), preferred_element_type=jnp.float32)

    return mm(high, left_high) + (mm(low, left_high) + mm(high, left_low))


def fold(x):
    h = x.shape[1] // 2
    return x[:, :h] + x[:, h:], x[:, :h] - x[:, h:]


def unfold(a, b):
    return jnp.concatenate([a + b, a - b], axis=1)


def lateral(x, even_ref, odd_ref, skew_ref):
    u, w = fold(x)
    uu, uw = fold(u)
    return unfold(unfold(times(uu, even_ref), times(uw, odd_ref)), times(w, skew_ref))


def lines_of(ref, lines):
    chunks = ref.shape[0] // lines
    return [ref[pl.ds(c, lines, stride=chunks), :] for c in range(chunks)]


def put_lines(ref, chunks):
    for c, value in enumerate(chunks):
        ref[pl.ds(c, value.shape[0], stride=len(chunks)), :] = value


def turned(chunks):
    return jnp.concatenate([v.T for v in chunks], axis=0)


def share_rows(depth, groups):
    shared = 2 * depth // (3 * groups)
    own = (depth - groups // 2 * shared) // groups
    assert own * groups + shared * (groups // 2) == depth
    return own, shared


def send_rows(own_ref, shared_ref, slot, field):
    groups, halves_ = own_ref.shape[0], shared_ref.shape[0]
    own, shared = share_rows(field.shape[0], groups)
    for d in range(groups):
        own_ref[d, slot * own : (slot + 1) * own, :] = field[d * own : (d + 1) * own]
    for r in range(halves_):
        start = groups * own + r * shared
        shared_ref[r, slot * shared : (slot + 1) * shared, :] = field[start : start + shared]


def spread(table, shape):
    return jnp.broadcast_to(jnp.pad(table, ((0, 0), (0, LANES - table.shape[1]))), shape)


def look_up(material, table):
    return jnp.take_along_axis(spread(table, material.shape), material, axis=1, mode="promise_in_bounds")


def interfaces_of(down, layers):
    depth = down.shape[0]
    packed = down.astype(jnp.float32).astype(jnp.bfloat16)
    blocks = [packed[i : i + 16] for i in range(0, depth, 16)]
    reach = 256 // (layers - 1)
    totals = [0.0]
    for layer in range(1, layers):
        total = 0.0
        for first in range(0, len(blocks), reach):
            part = None
            for block in blocks[first : first + reach]:
                value = jnp.minimum(block, jnp.bfloat16(layer))
                part = value if part is None else part + value
            total = total + part.astype(jnp.float32)
        totals.append(jnp.sum(total, axis=0, keepdims=True))
    return [depth - (b - a) for a, b in zip(totals, totals[1:])]


def depth_pair(first, second, land, gram, inner_ref, outer_ref):
    lines = first[0].shape[0]
    both = jnp.concatenate(
        [jnp.concatenate(first, axis=1), jnp.concatenate(second, axis=1)], axis=0
    )
    pad = outer_ref.shape[1]
    top = times_t(both[:, :LANES], gram[: 2 * pad])
    bottom = times_t(both[:, both.shape[1] - LANES :], gram[2 * pad :])
    picked = jnp.concatenate([land, land], axis=0)[:, :pad]
    extension = jnp.where(picked, top[:, :pad], top[:, pad:]) + bottom
    out = times(both, inner_ref) + times(extension, outer_ref)

    def chunked(x):
        return [x[:, c * LANES : (c + 1) * LANES] for c in range(len(first))]

    return chunked(out[:lines]), chunked(out[lines:])


def gram_of(top_land_ref, top_sea_ref, bottom_ref, pad):
    def padded(ref, start):
        extra, window = ref.shape
        return jnp.pad(ref[...], ((0, pad - extra), (start, LANES - window - start)))

    return jnp.concatenate(
        [padded(top_land_ref, 0), padded(top_sea_ref, 0), padded(bottom_ref, LANES - bottom_ref.shape[1])], axis=0
    )


def land_of(land_ref):
    lines = land_ref.shape[1]
    return jnp.broadcast_to(land_ref[...], (LANES, lines)).T > 0


def first_kernel(
    place_ref, xz_hbm, zz_hbm, inner_hbm, xx_hbm, material_hbm, vx_hbm, vz_hbm, land_hbm, top_land_hbm, top_sea_hbm,
    bottom_hbm, outer_hbm, density_hbm, lame_hbm, shear_hbm, *rest,
):
    (*out_refs, fields, material_ref, inner_ref, land_ref, top_land_ref, top_sea_ref, bottom_ref, outer_ref,
     density_ref, lame_ref, shear_ref, packed, shared, sems) = rest
    groups = packed.shape[0]
    lines = land_ref.shape[1]
    layers = density_ref.shape[1]
    moves = (
        (xz_hbm, fields.at[0]),
        (zz_hbm, fields.at[1]),
        (xx_hbm, fields.at[2]),
        (vx_hbm, fields.at[3]),
        (vz_hbm, fields.at[4]),
        (material_hbm, material_ref),
        (inner_hbm, inner_ref),
        (land_hbm, land_ref),
        (top_land_hbm, top_land_ref),
        (top_sea_hbm, top_sea_ref),
        (bottom_hbm, bottom_ref),
        (outer_hbm, outer_ref),
        (density_hbm, density_ref),
        (lame_hbm, lame_ref),
        (shear_hbm, shear_ref),
    )
    copies = [pltpu.make_async_copy(a, b, sems.at[i]) for i, (a, b) in enumerate(moves)]
    for i in (7, 8, 9, 10, 11, 12, 13, 14, 0, 1, 6, 5, 3, 4, 2):
        copies[i].start()
    for i in range(7, 15):
        copies[i].wait()
    gram = gram_of(top_land_ref, top_sea_ref, bottom_ref, outer_ref.shape[1])
    land = land_of(land_ref)
    for i in (0, 1, 6, 5):
        copies[i].wait()
    xz = lines_of(fields.at[0], lines)
    depth_xz, depth_zz = depth_pair(
        xz, lines_of(fields.at[1], lines), land, gram, inner_ref, outer_ref
    )
    send_rows(packed, shared, 1, turned(xz))
    material = lines_of(material_ref, lines)
    down = turned(material)
    counts = interfaces_of(down, layers)
    own = 4 * share_rows(down.shape[0], groups)[0]
    rows = packed.shape[1] - own
    counts = jnp.concatenate(counts + [counts[-1]] * (rows - layers + 1), axis=0)
    for d in range(groups):
        packed[d, own:, :] = counts
    table = time_step * (1.0 / density_ref[...])
    step = [look_up(m, table) for m in material]
    copies[2].wait()
    copies[3].wait()
    copies[4].wait()
    send_rows(packed, shared, 0, turned(lines_of(fields.at[2], lines)))
    for slot, i, d in ((2, 3, depth_xz), (3, 4, depth_zz)):
        mixed = [v + s * x for v, s, x in zip(lines_of(fields.at[i], lines), step, d)]
        send_rows(packed, shared, slot, turned(mixed))
    place, half = place_ref[0], groups // 2
    near, far, far_shared, land_out = out_refs[:half], out_refs[half:groups], out_refs[groups:-3], out_refs[-3]
    land_out[...] = land.astype(jnp.float32)
    out_refs[-2][...] = gram
    lame, shear = lame_ref[...], shear_ref[...]
    for i, row in enumerate((time_step * lame, time_step * (lame + 2.0 * shear), time_step * shear)):
        out_refs[-1][i : i + 1, :] = jnp.pad(row, ((0, 0), (0, LANES - layers)))
    for s, ref in enumerate(near):
        ref[: packed.shape[1], :] = packed[place ^ s]
        ref[packed.shape[1] :, :] = shared[(place ^ s) & (half - 1)]
    for s, ref in enumerate(far):
        ref[...] = packed[place ^ (s + half)]
    for s, ref in enumerate(far_shared):
        ref[...] = shared[(place ^ s) & (half - 1)]


def step_of(interfaces, depth, step_ref):
    step = jnp.full(depth.shape, step_ref[0], jnp.float32)
    for layer in range(1, step_ref.shape[0]):
        step = jnp.where(depth >= interfaces[layer - 1 : layer], step_ref[layer], step)
    return jnp.concatenate([step, step], axis=0)


def pencil_kernel(groups, place_ref, step_ref, even_ref, odd_ref, skew_ref, *rest):
    in_refs, out_refs, (stress, slope, moving) = rest[:groups], rest[groups : 2 * groups], rest[2 * groups :]
    n = in_refs[0].shape[1]
    place = place_ref[0]
    w = stress.shape[1] // 2
    for s, ref in enumerate(in_refs):
        stress[place ^ s] = ref[: 2 * w]
    slopes = lateral(jnp.concatenate([stress[q] for q in range(groups)], axis=1), even_ref, odd_ref, skew_ref)
    for q in range(groups):
        slope[q] = slopes[:, q * n : (q + 1) * n]
    depth = (lax.broadcasted_iota(jnp.int32, (w, n), 0) + place * w).astype(jnp.float32)
    for s, ref in enumerate(in_refs):
        step = step_of(ref[4 * w : 4 * w + step_ref.shape[0] - 1], depth, step_ref)
        new = ref[2 * w : 4 * w] + step * slope[place ^ s]
        out_refs[s][: 2 * w] = new
        moving[place ^ s] = new
    slopes = lateral(jnp.concatenate([moving[q] for q in range(groups)], axis=1), even_ref, odd_ref, skew_ref)
    for q in range(groups):
        slope[q] = slopes[:, q * n : (q + 1) * n]
    for s, ref in enumerate(out_refs):
        ref[2 * w :] = slope[place ^ s]


def shared_kernel(groups, base, place_ref, step_ref, even_ref, odd_ref, skew_ref, *rest):
    half = groups // 2
    near, far, far_shared = rest[:half], rest[half:groups], rest[groups : groups + half]
    done, out_refs, (stress, slope, moving) = rest[groups + half : 2 * groups], rest[2 * groups : -3], rest[-3:]
    n = near[0].shape[1]
    place = place_ref[0]
    w = stress.shape[1] // 2
    top = near[0].shape[0] - 4 * w
    rows = step_ref.shape[0] - 1
    held = top - -(-rows // 8) * 8
    blocks = [(s, ref, ref, top) for s, ref in enumerate(near)] + [
        (s + half, ref, raw, 0) for s, (ref, raw) in enumerate(zip(far, far_shared))
    ]
    for s, _, raw, start in blocks:
        stress[place ^ s] = raw[start : start + 2 * w]
    slopes = lateral(jnp.concatenate([stress[q] for q in range(groups)], axis=1), even_ref, odd_ref, skew_ref)
    for q in range(groups):
        slope[q] = slopes[:, q * n : (q + 1) * n]
    depth = lax.broadcasted_iota(jnp.int32, (w, n), 0) + base + (place & (half - 1)) * w
    depth = depth.astype(jnp.float32)
    for s, ref, raw, start in blocks:
        step = step_of(ref[held : held + rows], depth, step_ref)
        new = raw[start + 2 * w : start + 4 * w] + step * slope[place ^ s]
        if s < half:
            out_refs[s][done[s].shape[0] : done[s].shape[0] + 2 * w] = new
        moving[place ^ s] = new
    slopes = lateral(jnp.concatenate([moving[q] for q in range(groups)], axis=1), even_ref, odd_ref, skew_ref)
    for q in range(groups):
        slope[q] = slopes[:, q * n : (q + 1) * n]
    for s, ref in enumerate(out_refs):
        ref[: done[s].shape[0]] = done[s][...]
        ref[done[s].shape[0] + 2 * w :] = slope[place ^ s]


def gather_rows(own_ref, shared_ref, slot):
    own, shared = own_ref.shape[1] // 4, shared_ref.shape[1] // 4
    field = jnp.concatenate(
        [own_ref[d, slot * own : (slot + 1) * own, :] for d in range(own_ref.shape[0])]
        + [shared_ref[r, slot * shared : (slot + 1) * shared, :] for r in range(shared_ref.shape[0])],
        axis=0,
    )
    return [field[c * LANES : (c + 1) * LANES].T for c in range(field.shape[0] // LANES)]


def last_kernel(
    groups, place_ref, xx_ref, zz_ref, xz_ref, material_ref, inner_ref, outer_ref, land_ref, gram_ref, table_ref,
    *rest,
):
    in_refs = rest[:groups]
    new_vx, new_vz, new_xx_ref, new_zz_ref, new_xz_ref, settled, settled_shared = rest[groups:]
    lines = land_ref.shape[0]
    place, half, rows = place_ref[0], groups // 2, settled.shape[1]
    for s, ref in enumerate(in_refs):
        settled[place ^ s] = ref[:rows]
    for s, ref in enumerate(in_refs[:half]):
        settled_shared[(place ^ s) & (half - 1)] = ref[rows:]
    land = land_ref[...] > 0
    gram = gram_ref[...]
    vx, vz, lateral_x, lateral_z = (gather_rows(settled, settled_shared, i) for i in range(4))
    put_lines(new_vx, vx)
    put_lines(new_vz, vz)
    dx, dz = depth_pair(vx, vz, land, gram, inner_ref, outer_ref)
    results = ([], [], [])
    tables = [table_ref[i : i + 1, :] for i in range(3)]
    xx, zz, xz = lines_of(xx_ref, lines), lines_of(zz_ref, lines), lines_of(xz_ref, lines)
    material = lines_of(material_ref, lines)
    for c in range(len(vx)):
        lame, normal, shear = (look_up(material[c], table) for table in tables)
        new_xx = xx[c] + (normal * lateral_x[c] + lame * dz[c])
        new_zz = zz[c] + (lame * lateral_x[c] + normal * dz[c])
        new_xz = xz[c] + shear * (dx[c] + lateral_z[c])
        if c == 0:
            surface = lax.broadcasted_iota(jnp.int32, new_zz.shape, 1) == 0
            new_zz = jnp.where(surface & land, 0.0, new_zz)
            new_xz = jnp.where(surface, 0.0, new_xz)
        for kept, value in zip(results, (new_xx, new_zz, new_xz)):
            kept.append(value)
    for ref, value in zip((new_xx_ref, new_zz_ref, new_xz_ref), results):
        put_lines(ref, value)


def call(kernel, outs, specs, args, flops, scratch=(), on_chip=True):
    moved = sum(a.size * a.dtype.itemsize for a in (*args, *outs))
    return pl.pallas_call(
        kernel,
        out_shape=tuple(pltpu.VMEM(o.shape, o.dtype) if on_chip else o for o in outs),
        in_specs=list(specs),
        out_specs=(VMEM,) * len(outs),
        scratch_shapes=list(scratch),
        cost_estimate=pl.CostEstimate(flops=flops, bytes_accessed=moved, transcendentals=0),
        compiler_params=pltpu.CompilerParams(vmem_limit_bytes=16 << 20),
    )(*args)


def hop(blocks, groups):
    moved = {}
    for s, block in blocks.items():
        moved[s] = lax.ppermute(block, "gx", [(i, i ^ s) for i in range(groups)])
    return moved


def body(
    groups,
    velocity_x,
    velocity_z,
    stress_xx,
    stress_zz,
    stress_xz,
    material,
    land_mask,
    density,
    lame_lambda,
    shear_modulus,
    continuation_land,
    continuation_sea,
    continuation_bottom,
):
    lines, _, depth = velocity_x.shape
    width = lines * groups
    extra = continuation_land.shape[0]
    layers = density.shape[0]
    own, shared = share_rows(depth, groups)
    half = groups // 2
    f32 = jnp.float32

    def shape(*dims):
        return jax.ShapeDtypeStruct(dims, f32)

    def kept(x):
        return pltpu.with_memory_space_constraint(x, pltpu.HBM)

    def flat(x):
        return x.reshape(lines * depth // LANES, LANES)

    vx, vz, xx, zz, xz, material = map(
        flat, (velocity_x, velocity_z, stress_xx, stress_zz, stress_xz, material)
    )
    land = land_mask.reshape(1, lines)
    inner, outer = depth_constants(depth, extra)
    fold_matrices = lateral_constants(width)
    grams = (continuation_land, continuation_sea, continuation_bottom)
    step = time_step * (1.0 / density)
    place = lax.axis_index("gx").astype(jnp.int32).reshape(1)
    rows = -(-(layers - 1) // 8) * 8
    depth_flops = 2 * 2 * lines * depth * depth * 3
    lateral_flops = 2 * 2 * own * width * width
    stored = vx.shape

    near = range(half)
    far = range(half, groups)
    sent = call(
        first_kernel,
        [shape(4 * own + rows + 4 * shared, lines)] * half
        + [shape(4 * own + rows, lines)] * half
        + [shape(4 * shared, lines)] * half
        + [shape(lines, LANES), shape(3 * outer.shape[1], LANES), shape(8, LANES)],
        [SMEM] + [HBM] * 15,
        (place, *map(kept, (xz, zz, inner, xx, material, vx, vz, land, *grams, outer, *(t.reshape(1, layers) for t in (density, lame_lambda, shear_modulus))))),
        depth_flops,
        [
            pltpu.VMEM((5, *stored), f32),
            pltpu.VMEM(stored, jnp.int32),
            pltpu.VMEM(inner.shape, inner.dtype),
            pltpu.VMEM(land.shape, jnp.int32),
            *(pltpu.VMEM(g.shape, f32) for g in grams),
            pltpu.VMEM(outer.shape, outer.dtype),
            *[pltpu.VMEM((1, layers), f32)] * 3,
            pltpu.VMEM((groups, 4 * own + rows, lines), f32),
            pltpu.VMEM((half, 4 * shared, lines), f32),
            pltpu.SemaphoreType.DMA((15,)),
        ],
    )
    got = hop({s: sent[s] for s in range(1, groups)}, groups)
    raw = hop({s: sent[s + half] for s in far}, groups)
    got[0] = sent[0]
    ready = call(
        functools.partial(pencil_kernel, groups),
        [shape(4 * own, lines)] * groups,
        [SMEM] * 2 + [VMEM] * (3 + groups),
        (place, step, *fold_matrices, *(got[s] for s in range(groups))),
        2 * lateral_flops,
        [pltpu.VMEM((groups, 2 * own, lines), f32)] * 3,
    )
    back = hop({s: ready[s] for s in far}, groups)
    joined = call(
        functools.partial(shared_kernel, groups, groups * own),
        [shape(4 * own + 4 * shared, lines)] * half,
        [SMEM] * 2 + [VMEM] * (3 + 2 * groups),
        (
            place,
            step,
            *fold_matrices,
            *(got[s] for s in range(groups)),
            *(raw[s] for s in far),
            *(ready[s] for s in near),
        ),
        2 * lateral_flops,
        [pltpu.VMEM((groups, 2 * shared, lines), f32)] * 3,
    )
    back |= hop({s: joined[s] for s in range(1, half)}, groups)
    back[0] = joined[0]
    results = call(
        functools.partial(last_kernel, groups),
        [shape(*stored)] * 5,
        [SMEM] + [VMEM] * (9 + groups),
        (
            place,
            xx,
            zz,
            xz,
            material,
            inner,
            outer,
            *sent[-3:],
            *(back[s] for s in range(groups)),
        ),
        depth_flops,
        [pltpu.VMEM((groups, 4 * own, lines), f32), pltpu.VMEM((half, 4 * shared, lines), f32)],
        False,
    )
    return tuple(x.reshape(velocity_x.shape) for x in results)


def solution(mesh):
    field = P("gx", "gy", None)
    groups = mesh.shape["gx"]


    return jax.shard_map(
        functools.partial(body, groups),
        mesh=mesh,
        in_specs=(field,) * 6 + (P("gx", "gy"),) + (P(),) * 6,
        out_specs=(field,) * 5,
        check_vma=False,
    )
```

```python
import functools

import jax
import jax.numpy as jnp
import numpy as np
from jax import lax
from jax.experimental import pallas as pl
from jax.experimental.pallas import tpu as pltpu
from jax.sharding import PartitionSpec as P


time_step = 0.2
LANES = 128
VMEM = pl.BlockSpec(memory_space=pltpu.VMEM)
SMEM = pl.BlockSpec(memory_space=pltpu.SMEM)
HBM = pl.BlockSpec(memory_space=pltpu.HBM)


def circulant_row(length):
    m = np.arange(length)
    m = np.where(m < length - length // 2, m, m - length)
    angle = np.pi * m / length
    tangent = np.where(m == 0, 1.0, np.tan(angle))
    return np.where(m == 0, 0.0, (1.0 - 2.0 * (m % 2)) * (np.pi / length) / tangent)


def halves(matrix):
    matrix = matrix.astype(np.float32)
    high = matrix.astype(jnp.bfloat16)
    low = (matrix - high.astype(np.float32)).astype(jnp.bfloat16)
    return jnp.asarray(np.stack([high, low]))


def lateral_constants(length):
    c = circulant_row(length)

    def block(first, second, sign, scale):
        n = len(first)
        d = np.arange(n)[None, :] - np.arange(n)[:, None]
        value = first + sign * second
        entry = value[d % n]
        return scale * (entry if sign > 0 else np.where(d < 0, -entry, entry))

    h = length // 2
    skew_half = block(c[:h], c[h:], -1, 0.5)
    u = c[:h] + c[h:]
    q = h // 2
    return (
        halves(block(u[:q], u[q:], 1, 0.25)),
        halves(block(u[:q], u[q:], -1, 0.25)),
        halves(skew_half),
    )


def depth_constants(depth, extra):
    c = circulant_row(depth + extra)
    j, k = np.arange(depth), np.arange(depth + extra)
    matrix = c[(j[:, None] - k[None, :]) % (depth + extra)]
    h = depth // 2
    straight, mirrored = matrix[:h, :h], matrix[:h, h:depth][:, ::-1]
    pad = -(-extra // 32) * 32
    boundary = np.zeros((depth, pad))
    boundary[:, :extra] = matrix[:, depth:]
    inner = np.stack([0.5 * (straight + mirrored), 0.5 * (straight - mirrored)])
    return halves(inner).reshape(4, h, h), halves(boundary)


def split(x):
    high = x.astype(jnp.bfloat16)
    return high, (x - high.astype(jnp.float32)).astype(jnp.bfloat16)


def times(x, right):
    high, low = split(x)

    def mm(a, b):
        return jnp.dot(a, b, preferred_element_type=jnp.float32)

    rows = x.shape[0]
    stacked = mm(jnp.concatenate([high, low], axis=0), right[0])
    return stacked[:rows] + (stacked[rows:] + mm(high, right[1]))


def apply_left(left, x):
    high, low = split(x)

    def mm(a, b):
        return jnp.dot(a, b, preferred_element_type=jnp.float32)

    rows = left[0].shape[0]
    stacked = mm(jnp.concatenate([left[0], left[1]], axis=0), high)
    return stacked[:rows] + (stacked[rows:] + mm(left[0], low))


def reversed_rows(x):
    tiles = [x[i : i + 8] for i in range(0, x.shape[0], 8)][::-1]
    if x.shape[1] % LANES:
        tiles = [jnp.concatenate([t[i : i + 1] for i in range(7, -1, -1)], axis=0) for t in tiles]
    else:
        turn = 7 - lax.broadcasted_iota(jnp.int32, (8, x.shape[1]), 0)
        tiles = [jnp.take_along_axis(t, turn, axis=0, mode="promise_in_bounds") for t in tiles]
    return jnp.concatenate(tiles, axis=0)


def fold(x):
    h = x.shape[1] // 2
    return x[:, :h] + x[:, h:], x[:, :h] - x[:, h:]


def unfold(a, b):
    return jnp.concatenate([a + b, a - b], axis=1)


def lateral(x, even_ref, odd_ref, skew_ref):
    u, w = fold(x)
    uu, uw = fold(u)
    return unfold(unfold(times(uu, even_ref), times(uw, odd_ref)), times(w, skew_ref))


def lines_of(ref, lines):
    chunks = ref.shape[0] // lines
    return [ref[pl.ds(c, lines, stride=chunks), :] for c in range(chunks)]


def put_lines(ref, chunks):
    for c, value in enumerate(chunks):
        ref[pl.ds(c, value.shape[0], stride=len(chunks)), :] = value


def turned(chunks):
    return jnp.concatenate([v.T for v in chunks], axis=0)


def share_rows(depth, groups):
    shared = depth // (2 * groups)
    own = (depth - groups // 2 * shared) // groups
    assert own * groups + shared * (groups // 2) == depth
    return own, shared


def send_rows(own_ref, shared_ref, slot, field):
    groups, halves_ = own_ref.shape[0], shared_ref.shape[0]
    own, shared = share_rows(field.shape[0], groups)
    for d in range(groups):
        own_ref[d, slot * own : (slot + 1) * own, :] = field[d * own : (d + 1) * own]
    for r in range(halves_):
        start = groups * own + r * shared
        shared_ref[r, slot * shared : (slot + 1) * shared, :] = field[start : start + shared]


def look_up(material, table):
    lanes = material.shape[1]
    if lanes % LANES:
        value = jnp.broadcast_to(table[:, :1], material.shape)
        for layer in range(1, table.shape[1]):
            value = jnp.where(material == layer, table[:, layer : layer + 1], value)
        return value
    row = jnp.pad(table, ((0, 0), (0, lanes - table.shape[1]))) if table.shape[1] < lanes else table
    return jnp.take_along_axis(jnp.broadcast_to(row, material.shape), material, axis=1, mode="promise_in_bounds")


def interfaces_of(down, layers):
    depth = down.shape[0]
    packed = down.astype(jnp.float32).astype(jnp.bfloat16)
    blocks = [packed[i : i + 16] for i in range(0, depth, 16)]
    reach = 256 // (layers - 1)
    totals = [0.0]
    for layer in range(1, layers):
        total = 0.0
        for first in range(0, len(blocks), reach):
            part = None
            for block in blocks[first : first + reach]:
                value = jnp.minimum(block, jnp.bfloat16(layer))
                part = value if part is None else part + value
            total = total + part.astype(jnp.float32)
        totals.append(jnp.sum(total, axis=0, keepdims=True))
    return [depth - (b - a) for a, b in zip(totals, totals[1:])]


def depth_slope(x, land, gram, inner_ref, outer_ref):
    pad = outer_ref.shape[2]
    h = x.shape[0] // 2
    top = apply_left(split(gram[: 2 * pad]), x[:LANES])
    bottom = apply_left(split(gram[2 * pad :]), x[x.shape[0] - LANES :])
    extension = jnp.where(land, top[:pad], top[pad:]) + bottom
    upper, lower = x[:h], reversed_rows(x[h:])
    even = apply_left((inner_ref[0], inner_ref[2]), upper + lower)
    odd = apply_left((inner_ref[1], inner_ref[3]), upper - lower)
    return jnp.concatenate([even + odd, reversed_rows(odd - even)], axis=0) + apply_left(outer_ref, extension)


def gram_of(top_land_ref, top_sea_ref, bottom_ref, pad):
    def padded(ref, start):
        extra, window = ref.shape
        return jnp.pad(ref[...], ((0, pad - extra), (start, LANES - window - start)))

    return jnp.concatenate(
        [padded(top_land_ref, 0), padded(top_sea_ref, 0), padded(bottom_ref, LANES - bottom_ref.shape[1])], axis=0
    )


def land_of(land_ref):
    lines = land_ref.shape[1]
    return jnp.broadcast_to(land_ref[...], (LANES, lines)).T > 0


def first_kernel(
    place_ref, xz_hbm, zz_hbm, inner_hbm, xx_hbm, material_hbm, vx_hbm, vz_hbm, land_hbm, top_land_hbm, top_sea_hbm,
    bottom_hbm, outer_hbm, density_hbm, lame_hbm, shear_hbm, *rest,
):
    (*far, packed, shared, row_out, land_out, gram_out, table_out, fields, material_ref, inner_ref, land_ref,
     top_land_ref, top_sea_ref, bottom_ref, outer_ref, density_ref, lame_ref, shear_ref, sems) = rest
    small = (row_out, land_out, gram_out, table_out)
    groups = packed.shape[0]
    lines = land_ref.shape[1]
    layers = density_ref.shape[1]
    moves = (
        (xz_hbm, fields.at[0]),
        (zz_hbm, fields.at[1]),
        (xx_hbm, fields.at[2]),
        (vx_hbm, fields.at[3]),
        (vz_hbm, fields.at[4]),
        (material_hbm, material_ref),
        (inner_hbm, inner_ref),
        (land_hbm, land_ref),
        (top_land_hbm, top_land_ref),
        (top_sea_hbm, top_sea_ref),
        (bottom_hbm, bottom_ref),
        (outer_hbm, outer_ref),
        (density_hbm, density_ref),
        (lame_hbm, lame_ref),
        (shear_hbm, shear_ref),
    )
    copies = [pltpu.make_async_copy(a, b, sems.at[i]) for i, (a, b) in enumerate(moves)]
    for i in (5, 7, 8, 9, 10, 11, 12, 13, 14, 0, 1, 6, 2, 3, 4):
        copies[i].start()
    for i in range(7, 15):
        copies[i].wait()
    pad = outer_ref.shape[2]
    gram = gram_of(top_land_ref, top_sea_ref, bottom_ref, pad)
    land = land_of(land_ref)
    row = jnp.concatenate([land_ref[...], land_ref[...]], axis=1)
    copies[5].wait()
    down = turned(lines_of(material_ref, lines))
    counts = interfaces_of(down, layers)
    own = 4 * share_rows(down.shape[0], groups)[0]
    rows = packed.shape[1] - own
    counts = jnp.concatenate(counts + [counts[-1]] * (rows - layers + 1), axis=0)
    for d in range(groups):
        packed[d, own:, :] = counts
    for i in (0, 1, 2, 3, 4, 6):
        copies[i].wait()
    xz = turned(lines_of(fields.at[0], lines))
    both = jnp.concatenate([xz, turned(lines_of(fields.at[1], lines))], axis=1)
    slopes = depth_slope(both, jnp.broadcast_to(row, (pad, 2 * lines)) > 0, gram, inner_ref, outer_ref)
    send_rows(packed, shared, 1, xz)
    step = look_up(down, time_step * (1.0 / density_ref[...]))
    send_rows(packed, shared, 0, turned(lines_of(fields.at[2], lines)))
    for slot, i, slope in ((2, 3, slopes[:, :lines]), (3, 4, slopes[:, lines:])):
        send_rows(packed, shared, slot, turned(lines_of(fields.at[i], lines)) + step * slope)
    half = groups // 2
    row_out, land_out, gram_out, table_out = small
    row_out[...] = jnp.broadcast_to(row, (pad, 2 * lines)).astype(jnp.float32)
    land_out[...] = land.astype(jnp.float32)
    gram_out[...] = gram
    lame, shear = lame_ref[...], shear_ref[...]
    for i, line in enumerate((time_step * lame, time_step * (lame + 2.0 * shear), time_step * shear)):
        table_out[i : i + 1, :] = jnp.pad(line, ((0, 0), (0, LANES - layers)))
    for s, ref in enumerate(far):
        ref[...] = packed[place_ref[0] ^ (s + half), : ref.shape[0]]


def fill_kernel(groups, place_ref, packed, shared, *out_refs):
    half = groups // 2
    place = place_ref[0]
    near, far_shared = out_refs[:half], out_refs[half:]
    for s, ref in enumerate(near):
        ref[: packed.shape[1], :] = packed[place ^ s]
        ref[packed.shape[1] :, :] = shared[(place ^ s) & (half - 1)]
    for s, ref in enumerate(far_shared):
        ref[...] = shared[(place ^ s) & (half - 1)]


def step_of(interfaces, depth, step_ref):
    step = jnp.full(depth.shape, step_ref[0], jnp.float32)
    for layer in range(1, step_ref.shape[0]):
        step = jnp.where(depth >= interfaces[layer - 1 : layer], step_ref[layer], step)
    return jnp.concatenate([step, step], axis=0)


def pencil_kernel(groups, place_ref, step_ref, even_ref, odd_ref, skew_ref, *rest):
    in_refs, out_refs, (stress, slope, moving) = rest[:groups], rest[groups : 2 * groups], rest[2 * groups :]
    n = in_refs[0].shape[1]
    place = place_ref[0]
    w = stress.shape[1] // 2
    for s, ref in enumerate(in_refs):
        stress[place ^ s] = ref[: 2 * w]
    slopes = lateral(jnp.concatenate([stress[q] for q in range(groups)], axis=1), even_ref, odd_ref, skew_ref)
    for q in range(groups):
        slope[q] = slopes[:, q * n : (q + 1) * n]
    depth = (lax.broadcasted_iota(jnp.int32, (w, n), 0) + place * w).astype(jnp.float32)
    for s, ref in enumerate(in_refs):
        step = step_of(ref[4 * w : 4 * w + step_ref.shape[0] - 1], depth, step_ref)
        new = ref[2 * w : 4 * w] + step * slope[place ^ s]
        out_refs[s][: 2 * w] = new
        moving[place ^ s] = new
    slopes = lateral(jnp.concatenate([moving[q] for q in range(groups)], axis=1), even_ref, odd_ref, skew_ref)
    for q in range(groups):
        slope[q] = slopes[:, q * n : (q + 1) * n]
    for s, ref in enumerate(out_refs):
        ref[2 * w :] = slope[place ^ s]


def shared_kernel(groups, base, place_ref, step_ref, even_ref, odd_ref, skew_ref, *rest):
    half = groups // 2
    near, far, far_shared = rest[:half], rest[half:groups], rest[groups : groups + half]
    done, out_refs, (stress, slope, moving) = rest[groups + half : 2 * groups], rest[2 * groups : -3], rest[-3:]
    n = near[0].shape[1]
    place = place_ref[0]
    w = stress.shape[1] // 2
    top = near[0].shape[0] - 4 * w
    rows = step_ref.shape[0] - 1
    held = top - -(-rows // 8) * 8
    blocks = [(s, ref, ref, top) for s, ref in enumerate(near)] + [
        (s + half, ref, raw, 0) for s, (ref, raw) in enumerate(zip(far, far_shared))
    ]
    for s, _, raw, start in blocks:
        stress[place ^ s] = raw[start : start + 2 * w]
    slopes = lateral(jnp.concatenate([stress[q] for q in range(groups)], axis=1), even_ref, odd_ref, skew_ref)
    for q in range(groups):
        slope[q] = slopes[:, q * n : (q + 1) * n]
    depth = lax.broadcasted_iota(jnp.int32, (w, n), 0) + base + (place & (half - 1)) * w
    depth = depth.astype(jnp.float32)
    for s, ref, raw, start in blocks:
        step = step_of(ref[held : held + rows], depth, step_ref)
        new = raw[start + 2 * w : start + 4 * w] + step * slope[place ^ s]
        if s < half:
            out_refs[s][done[s].shape[0] : done[s].shape[0] + 2 * w] = new
        moving[place ^ s] = new
    slopes = lateral(jnp.concatenate([moving[q] for q in range(groups)], axis=1), even_ref, odd_ref, skew_ref)
    for q in range(groups):
        slope[q] = slopes[:, q * n : (q + 1) * n]
    for s, ref in enumerate(out_refs):
        ref[: done[s].shape[0]] = done[s][...]
        ref[done[s].shape[0] + 2 * w :] = slope[place ^ s]


def gather_rows(own_ref, shared_ref, slot):
    own, shared = own_ref.shape[1] // 4, shared_ref.shape[1] // 4
    return jnp.concatenate(
        [own_ref[d, slot * own : (slot + 1) * own, :] for d in range(own_ref.shape[0])]
        + [shared_ref[r, slot * shared : (slot + 1) * shared, :] for r in range(shared_ref.shape[0])],
        axis=0,
    )


def lines_again(field):
    return [field[c : c + LANES].T for c in range(0, field.shape[0], LANES)]


def last_kernel(
    groups, place_ref, xx_ref, zz_ref, xz_ref, material_ref, inner_ref, outer_ref, land_row_ref, land_ref, gram_ref,
    table_ref, *rest,
):
    in_refs = rest[:groups]
    new_vx, new_vz, new_xx_ref, new_zz_ref, new_xz_ref, settled, settled_shared = rest[groups:]
    lines = land_ref.shape[0]
    place, half, rows = place_ref[0], groups // 2, settled.shape[1]
    for s, ref in enumerate(in_refs):
        settled[place ^ s] = ref[:rows]
    for s, ref in enumerate(in_refs[:half]):
        settled_shared[(place ^ s) & (half - 1)] = ref[rows:]
    vx, vz, lateral_x, lateral_z = (gather_rows(settled, settled_shared, i) for i in range(4))
    slopes = depth_slope(
        jnp.concatenate([vx, vz], axis=1),
        land_row_ref[...] > 0,
        gram_ref[...],
        inner_ref,
        outer_ref,
    )
    put_lines(new_vx, lines_again(vx))
    put_lines(new_vz, lines_again(vz))
    lateral_x, dz = lines_again(lateral_x), lines_again(slopes[:, lines:])
    shearing = lines_again(slopes[:, :lines] + lateral_z)
    land = land_ref[...] > 0
    results = ([], [], [])
    tables = [table_ref[i : i + 1, :] for i in range(3)]
    xx, zz, xz = lines_of(xx_ref, lines), lines_of(zz_ref, lines), lines_of(xz_ref, lines)
    material = lines_of(material_ref, lines)
    for c in range(len(dz)):
        lame, normal, shear = (look_up(material[c], table) for table in tables)
        new_xx = xx[c] + (normal * lateral_x[c] + lame * dz[c])
        new_zz = zz[c] + (lame * lateral_x[c] + normal * dz[c])
        new_xz = xz[c] + shear * shearing[c]
        if c == 0:
            surface = lax.broadcasted_iota(jnp.int32, new_zz.shape, 1) == 0
            new_zz = jnp.where(surface & land, 0.0, new_zz)
            new_xz = jnp.where(surface, 0.0, new_xz)
        for kept, value in zip(results, (new_xx, new_zz, new_xz)):
            kept.append(value)
    for ref, value in zip((new_xx_ref, new_zz_ref, new_xz_ref), results):
        put_lines(ref, value)


def call(kernel, outs, specs, args, flops, scratch=(), on_chip=True):
    moved = sum(a.size * a.dtype.itemsize for a in (*args, *outs))
    return pl.pallas_call(
        kernel,
        out_shape=tuple(pltpu.VMEM(o.shape, o.dtype) if on_chip else o for o in outs),
        in_specs=list(specs),
        out_specs=(VMEM,) * len(outs),
        scratch_shapes=list(scratch),
        cost_estimate=pl.CostEstimate(flops=flops, bytes_accessed=moved, transcendentals=0),
        compiler_params=pltpu.CompilerParams(vmem_limit_bytes=16 << 20),
    )(*args)


def hop(blocks, groups):
    moved = {}
    for s, block in blocks.items():
        moved[s] = lax.ppermute(block, "gx", [(i, i ^ s) for i in range(groups)])
    return moved


def body(
    groups,
    velocity_x,
    velocity_z,
    stress_xx,
    stress_zz,
    stress_xz,
    material,
    land_mask,
    density,
    lame_lambda,
    shear_modulus,
    continuation_land,
    continuation_sea,
    continuation_bottom,
):
    lines, _, depth = velocity_x.shape
    width = lines * groups
    extra = continuation_land.shape[0]
    layers = density.shape[0]
    own, shared = share_rows(depth, groups)
    half = groups // 2
    f32 = jnp.float32

    def shape(*dims):
        return jax.ShapeDtypeStruct(dims, f32)

    def kept(x):
        return pltpu.with_memory_space_constraint(x, pltpu.HBM)

    def flat(x):
        return x.reshape(lines * depth // LANES, LANES)

    vx, vz, xx, zz, xz, material = map(
        flat, (velocity_x, velocity_z, stress_xx, stress_zz, stress_xz, material)
    )
    land = land_mask.reshape(1, lines)
    inner, outer = depth_constants(depth, extra)
    fold_matrices = lateral_constants(width)
    grams = (continuation_land, continuation_sea, continuation_bottom)
    step = time_step * (1.0 / density)
    place = lax.axis_index("gx").astype(jnp.int32).reshape(1)
    rows = -(-(layers - 1) // 8) * 8
    depth_flops = 2 * 2 * lines * depth * depth * 3
    lateral_flops = 2 * 2 * own * width * width
    stored = vx.shape

    near = range(half)
    far = range(half, groups)
    sent = call(
        first_kernel,
        [shape(4 * own + rows, lines)] * half
        + [shape(groups, 4 * own + rows, lines), shape(half, 4 * shared, lines)]
        + [shape(outer.shape[2], 2 * lines), shape(lines, LANES), shape(3 * outer.shape[2], LANES), shape(8, LANES)],
        [SMEM] + [HBM] * 15,
        (place, *map(kept, (xz, zz, inner, xx, material, vx, vz, land, *grams, outer, *(t.reshape(1, layers) for t in (density, lame_lambda, shear_modulus))))),
        depth_flops,
        [
            pltpu.VMEM((5, *stored), f32),
            pltpu.VMEM(stored, jnp.int32),
            pltpu.VMEM(inner.shape, inner.dtype),
            pltpu.VMEM(land.shape, jnp.int32),
            *(pltpu.VMEM(g.shape, f32) for g in grams),
            pltpu.VMEM(outer.shape, outer.dtype),
            *[pltpu.VMEM((1, layers), f32)] * 3,
            pltpu.SemaphoreType.DMA((15,)),
        ],
    )
    filled = call(
        functools.partial(fill_kernel, groups),
        [shape(4 * own + rows + 4 * shared, lines)] * half + [shape(4 * shared, lines)] * half,
        [SMEM] + [VMEM] * 2,
        (place, sent[half], sent[half + 1]),
        0,
    )
    got = hop({s: sent[s - half] for s in far}, groups)
    got |= hop({s: filled[s] for s in range(1, half)}, groups)
    raw = hop({s: filled[s] for s in far}, groups)
    got[0] = filled[0]
    ready = call(
        functools.partial(pencil_kernel, groups),
        [shape(4 * own, lines)] * groups,
        [SMEM] * 2 + [VMEM] * (3 + groups),
        (place, step, *fold_matrices, *(got[s] for s in range(groups))),
        2 * lateral_flops,
        [pltpu.VMEM((groups, 2 * own, lines), f32)] * 3,
    )
    back = hop({s: ready[s] for s in far}, groups)
    joined = call(
        functools.partial(shared_kernel, groups, groups * own),
        [shape(4 * own + 4 * shared, lines)] * half,
        [SMEM] * 2 + [VMEM] * (3 + 2 * groups),
        (
            place,
            step,
            *fold_matrices,
            *(got[s] for s in range(groups)),
            *(raw[s] for s in far),
            *(ready[s] for s in near),
        ),
        2 * lateral_flops,
        [pltpu.VMEM((groups, 2 * shared, lines), f32)] * 3,
    )
    back |= hop({s: joined[s] for s in range(1, half)}, groups)
    back[0] = joined[0]
    results = call(
        functools.partial(last_kernel, groups),
        [shape(*stored)] * 5,
        [SMEM] + [VMEM] * (10 + groups),
        (
            place,
            xx,
            zz,
            xz,
            material,
            inner,
            outer,
            *sent[-4:],
            *(back[s] for s in range(groups)),
        ),
        depth_flops,
        [pltpu.VMEM((groups, 4 * own, lines), f32), pltpu.VMEM((half, 4 * shared, lines), f32)],
        False,
    )
    return tuple(x.reshape(velocity_x.shape) for x in results)


def solution(mesh):
    field = P("gx", "gy", None)
    groups = mesh.shape["gx"]


    return jax.shard_map(
        functools.partial(body, groups),
        mesh=mesh,
        in_specs=(field,) * 6 + (P("gx", "gy"),) + (P(),) * 6,
        out_specs=(field,) * 5,
        check_vma=False,
    )
```
